256 devices in a mesh: sx: 8 (over z), sy: 32 (over y, x, core).
Axes of the slice: x: 4, y: 4, z: 8, core: 2. Of those that a mesh axis runs over, the one named last changes fastest.
Arguments:
- loads: float32 [12288, 4096], P('sx', 'sy'), may hold values from -6 to 6
- dual_op: bfloat16 [12288, 49152], P('sx', 'sy'), as said below
- dirichlet: bfloat16 [12288, 49152], P('sx', 'sy'), as said below
- corner_coupling: bfloat16 [128, 49152], P('sx', 'sy'), may hold values from -0.625 to 0.625
- corner_map: int32 [8, 512], P('sx', 'sy'), may hold values from 0 to 2047, as said below
- coarse_inverse: float32 [2048, 2048], P('sy'), as said below
Outputs:
- multipliers: float32 [12288, 4096], P('sx', 'sy')
- residual: float32 [12288, 4096], P('sx', 'sy')
The draws below stay inside these ranges and needn't reach their ends.
Inputs may be any that keep to these rules, and one draw needn't show every extreme that they name: `corner_map`: every coarse unknown is named by exactly two entries over all subdomains. `dual_op`: each subdomain's block is symmetric positive definite. `dirichlet`: each subdomain's block is symmetric positive definite. `coarse_inverse`: symmetric positive definite.
All inputs are finite; a program needn't handle non-finite values.
Results may differ from the reference program's by a relative error of at most 0.014.
Values sent between devices are 32-bit elements; how exact they have to be, the bound alone decides.
No kernel may reach another device: no remote copies, remote signals or barrier semaphores. Data moves between devices by JAX's collectives and lax.ppermute only.
A program may use at most 64 MiB of HBM per device.

```python
import math
import jax
import jax.numpy as jnp
from jax import lax

FACE = 320
EDGE = 64
M = 1536
CORN_DEV = 16
CASES = 128
ITERS = 4
GRID_X = 8
GRID_Y = 32
NCOARSE = 2048


def definite_block(key, order, spread_low, spread_high, weight):
    first, second = jax.random.split(key)
    noise = jax.random.normal(first, (order, order), jnp.float32)
    symmetric = (noise + noise.T) * (weight / math.sqrt(2.0 * order))
    diagonal = jax.random.uniform(second, (order,), jnp.float32, spread_low, spread_high)
    return symmetric + jnp.diag(diagonal)


def definite_grid(key):
    keys = jax.random.split(key, GRID_X * GRID_Y)
    blocks = lax.map(lambda single: definite_block(single, M, 1.0, 2.0, 0.35).astype(jnp.bfloat16), keys)
    return blocks.reshape(GRID_X, GRID_Y, M, M).transpose(0, 2, 1, 3).reshape(GRID_X * M, GRID_Y * M)


def draw_dual_op(key, part):
    return definite_grid(jax.random.fold_in(key, 11))


def draw_dirichlet(key, part):
    return definite_grid(jax.random.fold_in(key, 12))


def draw_coarse_inverse(key, part):
    return definite_block(jax.random.fold_in(key, 13), NCOARSE, 0.5, 1.5, 0.3)


def draw_corner_map(key, part):
    folded = jax.random.fold_in(key, 14)
    first, second = jax.random.split(folded)
    labels = jnp.concatenate([jax.random.permutation(first, NCOARSE), jax.random.permutation(second, NCOARSE)])
    return labels.astype(jnp.int32).reshape(GRID_X, GRID_Y * CORN_DEV)


def block_levels(key, dims, cuts, smallest, high):
    gain = 1.0
    for position, shards_of in cuts:
        draws = jax.random.uniform(jax.random.fold_in(jax.random.fold_in(key, 6), position), (shards_of,), jnp.float32, smallest / len(cuts), high / len(cuts))
        gain = gain * jnp.repeat(jnp.exp(draws), dims[position] // shards_of).reshape((-1,) + (1,) * (len(dims) - 1 - position))
    return gain


def centred(rng, extent, scale, reach, shards=(), kind=jnp.bfloat16):
    drawn = scale * jax.random.normal(rng, extent, jnp.float32)
    if shards:
        drawn = drawn * block_levels(rng, extent, shards, -0.22, 0.18)
    return jnp.clip(drawn, -reach, reach).astype(kind)


def setup_inputs(seed: int = 0) -> dict:
    key_of = jax.random.split(jax.random.key(seed), 7)
    loads = centred(key_of[0], (GRID_X * M, GRID_Y * CASES), 1.0, 6.0, ((0, 8), (1, 32)), jnp.float32)
    dual_op = draw_dual_op(jax.random.fold_in(key_of[6], 71), 0)
    dirichlet = draw_dirichlet(jax.random.fold_in(key_of[6], 71), 0)
    corner_coupling = centred(key_of[3], (GRID_X * CORN_DEV, GRID_Y * M), (M // CORN_DEV) ** -0.5, 0.625, ((0, 8), (1, 32)))
    corner_map = draw_corner_map(jax.random.fold_in(key_of[6], 71), 0)
    coarse_inverse = draw_coarse_inverse(jax.random.fold_in(key_of[6], 71), 0)
    return dict(loads=loads, dual_op=dual_op, dirichlet=dirichlet, corner_coupling=corner_coupling, corner_map=corner_map, coarse_inverse=coarse_inverse)


HALF = 0.5
HIGH = lax.Precision.HIGHEST
OFFSETS = ((-1, 0), (1, 0), (0, -1), (0, 1), (-1, -1), (-1, 1), (1, -1), (1, 1))


def to_grid(whole, rows):
    columns = whole.shape[1] // GRID_Y
    return whole.reshape(GRID_X, rows, GRID_Y, columns).transpose(0, 2, 1, 3)


def from_grid(blocks):
    return blocks.transpose(0, 2, 1, 3).reshape(GRID_X * blocks.shape[2], GRID_Y * blocks.shape[3])


def grid_shift(blocks, step_x, step_y):
    padded = jnp.pad(blocks, ((1, 1), (1, 1), (0, 0), (0, 0)))
    return padded[1 - step_x:1 - step_x + GRID_X, 1 - step_y:1 - step_y + GRID_Y]


def assemble(field):
    widths = [FACE, FACE, FACE, FACE, EDGE, EDGE, EDGE, EDGE]
    pieces = []
    start = 0
    for width in widths:
        pieces.append(field[:, :, start:start + width])
        start = start + width
    result = []
    for index, offset in enumerate(OFFSETS):
        mirror = OFFSETS.index((-offset[0], -offset[1]))
        result.append(pieces[index] + HALF * grid_shift(pieces[mirror], -offset[0], -offset[1]))
    return jnp.concatenate(result, axis=2)


def apply_blocks(matrix, vectors):
    order = vectors.shape[2]
    grid = matrix.reshape(GRID_X, order, GRID_Y, order)

    def one_row(pair):
        rows, block = pair
        return jnp.einsum("iyj,yjr->yir", rows.astype(jnp.float32), block.astype(jnp.float32), precision=HIGH)

    return lax.map(one_row, (grid, vectors))


def operate(direction, dual_op, coupling, selector, coarse_inverse):
    spread = assemble(direction)
    rounded = spread.astype(jnp.bfloat16)
    local = apply_blocks(dual_op, rounded)
    widened = coupling.astype(jnp.float32)
    corner_part = jnp.einsum("xykm,xymr->xykr", widened, rounded.astype(jnp.float32), precision=HIGH)
    coarse_sum = jnp.einsum("xykn,xykr->nr", selector, corner_part, precision=HIGH)
    solution = jnp.dot(coarse_inverse, coarse_sum, precision=HIGH)
    picked = jnp.einsum("xykn,nr->xykr", selector, solution, precision=HIGH)
    correction = jnp.einsum("xykm,xykr->xymr", widened, picked, precision=HIGH)
    return assemble(local + correction)


def inner(first, second):
    return jnp.sum(first * second, axis=(0, 1, 2))


def reference(loads, dual_op, dirichlet, corner_coupling, corner_map, coarse_inverse):
    right = to_grid(loads, M)
    coupling = to_grid(corner_coupling, CORN_DEV)
    labels = corner_map.reshape(GRID_X, GRID_Y, CORN_DEV)
    selector = (labels[..., None] == jnp.arange(NCOARSE, dtype=jnp.int32)).astype(jnp.float32)
    multipliers = jnp.zeros_like(right)
    residual = right
    smoothed = apply_blocks(dirichlet, residual.astype(jnp.bfloat16))
    direction = smoothed
    current = inner(residual, smoothed)
    for step in range(ITERS):
        image = operate(direction, dual_op, coupling, selector, coarse_inverse)
        alpha = current / inner(direction, image)
        multipliers = multipliers + alpha * direction
        residual = residual - alpha * image
        if step + 1 < ITERS:
            smoothed = apply_blocks(dirichlet, residual.astype(jnp.bfloat16))
            following = inner(residual, smoothed)
            direction = smoothed + (following / current) * direction
            current = following
    return from_grid(multipliers), from_grid(residual)
```

```python
import functools
import math

import jax
import jax.numpy as jnp
from jax import lax
from jax.experimental import pallas as pl
from jax.experimental.pallas import tpu as pltpu
from jax.sharding import Mesh
from jax.sharding import PartitionSpec as P

FACE = 320
EDGE = 64
TILE = 256
ITERS = 4
HALF = 0.5
HIGH = lax.Precision.HIGHEST
SY = ("y", "x", "c")
ALL = ("z", "y", "x", "c")
GATHER = ("z", "c")
SCATTER = ("y", "x")


def shifted(value, step_z, step):
    nz, ns = lax.axis_size("z"), lax.axis_size(SY)
    pairs = []
    for z in range(nz):
        for k in range(ns):
            target = (z + step) % nz * ns + k if step_z else z * ns + (k + step) % ns
            pairs.append((z * ns + k, target))
    return lax.ppermute(value, ALL, pairs)


def call(kernel, shapes, operands, smem=0, scratch=(), flops=1_000_000):
    out_shape = [jax.ShapeDtypeStruct(shape, jnp.float32) for shape in shapes]
    moved = 4 * sum(math.prod(shape) for shape in shapes) + sum(x.size * x.dtype.itemsize for x in operands)
    return pl.pallas_call(
        kernel,
        out_shape=out_shape,
        in_specs=[pl.BlockSpec(memory_space=pltpu.SMEM)] * smem
        + [pl.BlockSpec(memory_space=pltpu.VMEM)] * (len(operands) - smem),
        out_specs=[pl.BlockSpec(memory_space=pltpu.VMEM)] * len(shapes),
        scratch_shapes=list(scratch),
        compiler_params=pltpu.CompilerParams(vmem_limit_bytes=6 * 1024 * 1024),
        cost_estimate=pl.CostEstimate(flops=flops, bytes_accessed=moved, transcendentals=0),
    )(*operands)


def put_parts(parts_ref, rows, value):
    cases = value.shape[1]
    high = value.astype(jnp.bfloat16)
    parts_ref[rows, :cases] = high
    parts_ref[rows, cases:] = (value - high.astype(jnp.float32)).astype(jnp.bfloat16)


def multiplied(matrix_ref, parts_ref, out_ref, extra=None):
    order, cases = out_ref.shape

    def tile(i, carry):
        rows = pl.ds(pl.multiple_of(i * TILE, TILE), TILE)
        wide = jnp.dot(matrix_ref[rows, :], parts_ref[...], preferred_element_type=jnp.float32)
        total = wide[:, :cases] + wide[:, cases:]
        if extra is not None:
            total = total + extra(rows)
        out_ref[rows, :] = total
        return carry

    lax.fori_loop(0, order // TILE, tile, 0)


def put_sends(field_ref, up_ref, down_ref, left_ref, right_ref):
    up_ref[0:320, :] = field_ref[320:640, :]
    up_ref[320:448, :] = field_ref[1408:1536, :]
    down_ref[0:320, :] = field_ref[0:320, :]
    down_ref[320:448, :] = field_ref[1280:1408, :]
    left_ref[...] = field_ref[640:960, :]
    right_ref[...] = field_ref[960:1280, :]


def forward_kernel(from_down_ref, from_up_ref, left_ref, right_ref):
    left_ref[0:64, :] = from_up_ref[320:384, :]
    left_ref[64:128, :] = from_down_ref[320:384, :]
    right_ref[0:64, :] = from_up_ref[384:448, :]
    right_ref[64:128, :] = from_down_ref[384:448, :]


def incoming(flags_ref, down_ref, up_ref, left_ref, right_ref, edge_left_ref, edge_right_ref):
    down, up, left, right = (flags_ref[k] == 1 for k in range(4))
    pieces = (
        (0, 320, down, down_ref, 0),
        (320, 640, up, up_ref, 0),
        (640, 960, left, left_ref, 0),
        (960, 1280, right, right_ref, 0),
        (1280, 1344, jnp.logical_and(left, down), edge_left_ref, 64),
        (1344, 1408, jnp.logical_and(right, down), edge_right_ref, 64),
        (1408, 1472, jnp.logical_and(left, up), edge_left_ref, 0),
        (1472, 1536, jnp.logical_and(right, up), edge_right_ref, 0),
    )
    return [
        (slice(low, high), jnp.where(there, ref[start : start + high - low, :], 0.0))
        for low, high, there, ref, start in pieces
    ]


def smooth_kernel(field_ref, matrix_ref, out_ref, *rest):
    *send_refs, parts_ref = rest
    put_parts(parts_ref, slice(None), field_ref[...])
    multiplied(matrix_ref, parts_ref, out_ref)
    put_sends(out_ref, *send_refs)


def spread_kernel(
    flags_ref, field_ref, z1, z2, s1, s2, d1, d2, matrix_ref, coupling_ref, dots_ref,
    spread_ref, local_ref, sent_ref, parts_ref,
):
    cases = spread_ref.shape[1]
    received_refs = z1, z2, s1, s2, d1, d2
    for rows, theirs in incoming(flags_ref, *received_refs):
        value = field_ref[rows, :] + HALF * theirs
        spread_ref[rows, :] = value
        put_parts(parts_ref, rows, value)
    wide = jnp.dot(coupling_ref[...], parts_ref[...], preferred_element_type=jnp.float32)
    corner = wide[:, :cases] + wide[:, cases:]
    for k in range(sent_ref.shape[0]):
        sent_ref[k, 0:16, :] = corner
        sent_ref[k, 16:24, :] = dots_ref[...]
    multiplied(matrix_ref, parts_ref, local_ref)


def coarse_kernel(got_ref, block_ref, sent_ref):
    count = got_ref.shape[0]
    parts = jnp.concatenate([got_ref[k, 0:16, :] for k in (*range(0, count, 2), *range(1, count, 2))], axis=0)
    sums = got_ref[0, 16:24, :]
    for k in range(1, count):
        sums = sums + got_ref[k, 16:24, :]
    product = jnp.dot(block_ref[...], parts, precision=HIGH, preferred_element_type=jnp.float32)
    for k in range(sent_ref.shape[0]):
        sent_ref[k, 0:16, :] = product[16 * k : 16 * k + 16]
        sent_ref[k, 16:24, :] = sums


def image_kernel(
    first_step, got_ref, local_ref, coupling_ref, last_ref,
    image_ref, z1, z2, s1, s2, scalars_ref, wide_ref,
):
    send_refs = z1, z2, s1, s2
    total = got_ref[0]
    for k in range(1, got_ref.shape[0]):
        total = total + got_ref[k]
    picked = total[0:16]
    high = picked.astype(jnp.bfloat16).astype(jnp.float32)
    rest = picked - high
    middle = rest.astype(jnp.bfloat16).astype(jnp.float32)
    wide_ref[0:16, :] = high
    wide_ref[16:32, :] = middle
    wide_ref[32:48, :] = rest - middle
    pieces = wide_ref[...].astype(jnp.bfloat16)
    order = image_ref.shape[0]
    gamma, delta = total[16:17], total[17:18]
    if first_step:
        alpha = gamma / delta
        beta = jnp.zeros_like(gamma)
    else:
        beta = gamma / last_ref[1:2, :]
        alpha = gamma / (delta - beta * gamma / last_ref[0:1, :])
    scalars_ref[0:1, :] = alpha
    scalars_ref[1:2, :] = gamma
    scalars_ref[2:3, :] = beta
    scalars_ref[3:8, :] = jnp.zeros((5,) + gamma.shape[1:], jnp.float32)
    image_ref[...] = local_ref[...] + jnp.dot(coupling_ref[...], pieces, preferred_element_type=jnp.float32)
    put_sends(image_ref, *send_refs)


def inner(first, second):
    return jnp.sum(first * second, axis=0, keepdims=True)


def start_kernel(
    flags_ref, image_ref, z1, z2, s1, s2, d1, d2, r_ref, u_ref, matrix_ref,
    w_ref, dots_ref, m_ref, a1, a2, b1, b2, parts_ref,
):
    delta = 0.0
    received_refs = z1, z2, s1, s2, d1, d2
    send_refs = a1, a2, b1, b2
    for rows, theirs in incoming(flags_ref, *received_refs):
        value = image_ref[rows, :] + HALF * theirs
        w_ref[rows, :] = value
        put_parts(parts_ref, rows, value)
        delta = delta + inner(value, u_ref[rows, :])
    dots_ref[...] = jnp.zeros_like(dots_ref)
    dots_ref[0:1, :] = inner(r_ref[...], u_ref[...])
    dots_ref[1:2, :] = delta
    multiplied(matrix_ref, parts_ref, m_ref)
    put_sends(m_ref, *send_refs)


def step_kernel(
    flags_ref, image_ref, z1, z2, s1, s2, d1, d2, z_ref, w_ref, r_ref, u_ref, scalars_ref, matrix_ref,
    new_z_ref, new_w_ref, dots_ref, m_ref, a1, a2, b1, b2, parts_ref,
):
    alpha, beta = scalars_ref[0:1, :], scalars_ref[2:3, :]
    delta = 0.0
    received_refs = z1, z2, s1, s2, d1, d2
    send_refs = a1, a2, b1, b2
    for rows, theirs in incoming(flags_ref, *received_refs):
        z = image_ref[rows, :] + HALF * theirs + beta * z_ref[rows, :]
        new_z_ref[rows, :] = z
        value = w_ref[rows, :] - alpha * z
        new_w_ref[rows, :] = value
        put_parts(parts_ref, rows, value)
        delta = delta + inner(value, u_ref[rows, :])
    dots_ref[...] = jnp.zeros_like(dots_ref)
    dots_ref[0:1, :] = inner(r_ref[...], u_ref[...])
    dots_ref[1:2, :] = delta
    multiplied(matrix_ref, parts_ref, m_ref)
    put_sends(m_ref, *send_refs)


def update_kernel(
    scalars_ref, u_ref, w_ref, r_ref, x_ref, p_ref, s_ref, q_ref, m_ref, yu_ref, yq_ref, ym_ref,
    new_u, new_r, new_x, new_p, new_s, new_q, new_yu, new_yq,
):
    alpha, beta = scalars_ref[0:1, :], scalars_ref[2:3, :]

    def tile(i, carry):
        rows = pl.ds(pl.multiple_of(i * TILE, TILE), TILE)
        u = u_ref[rows, :]
        p = u + beta * p_ref[rows, :]
        s = w_ref[rows, :] + beta * s_ref[rows, :]
        q = m_ref[rows, :] + beta * q_ref[rows, :]
        yq = ym_ref[rows, :] + beta * yq_ref[rows, :]
        new_p[rows, :] = p
        new_s[rows, :] = s
        new_q[rows, :] = q
        new_yq[rows, :] = yq
        new_x[rows, :] = x_ref[rows, :] + alpha * p
        new_r[rows, :] = r_ref[rows, :] - alpha * s
        new_u[rows, :] = u - alpha * q
        new_yu[rows, :] = yu_ref[rows, :] - alpha * yq
        return carry

    lax.fori_loop(0, u_ref.shape[0] // TILE, tile, 0)


def ends_kernel(scalars_ref, u_ref, r_ref, w_ref, z_ref, yu_ref, image_ref, sent_ref):
    alpha, beta = scalars_ref[0:1, :], scalars_ref[2:3, :]
    u = u_ref[...]
    gamma = inner(r_ref[...], u)
    delta = inner(u, w_ref[...] - (alpha * beta) * z_ref[...]) - alpha * inner(yu_ref[...], image_ref[...])
    both = jnp.concatenate([gamma, delta], axis=0)
    sent_ref[...] = jnp.broadcast_to(both[None], sent_ref.shape)


def finish_kernel(flags_ref, image_ref, z1, z2, s1, s2, d1, d2, out_ref):
    received_refs = z1, z2, s1, s2, d1, d2
    for rows, theirs in incoming(flags_ref, *received_refs):
        out_ref[rows, :] = image_ref[rows, :] + HALF * theirs


def rounded_part(value):
    return lax.reduce_precision(value, exponent_bits=8, mantissa_bits=7)


def split3(value):
    high = rounded_part(value)
    middle = rounded_part(value - high)
    low = value - high - middle
    return high.astype(jnp.bfloat16), middle.astype(jnp.bfloat16), low.astype(jnp.bfloat16)


def picked_product(left_f32, onehot):
    rows = left_f32.shape[0]
    product = jnp.dot(jnp.concatenate(split3(left_f32), axis=0), onehot, preferred_element_type=jnp.float32)
    return product[:rows] + product[rows : 2 * rows] + product[2 * rows :]


def coarse_columns(corner_map, coarse_inverse):
    nz, ns = lax.axis_size("z"), lax.axis_size(SY)
    corners = corner_map.shape[1]
    rows, order = coarse_inverse.shape
    mine = jnp.pad(corner_map.astype(jnp.float32), ((0, 0), (0, 128 - corners)))
    sent = jnp.broadcast_to(mine[None], (nz * ns, 1, 128))
    maps = lax.all_to_all(sent, ALL, 0, 0)[:, 0, :corners].astype(jnp.int32).reshape(nz, ns, corners)
    columns = maps.transpose(1, 0, 2).reshape(ns * nz * corners)
    iota = lax.broadcasted_iota(jnp.int32, (order, 1), 0)
    onehot = (iota == columns[None, :]).astype(jnp.bfloat16)
    chosen = picked_product(coarse_inverse, onehot)
    return maps, chosen.reshape(rows, ns, nz * corners).transpose(1, 0, 2)


def coarse_block(maps, got):
    ns, corners = maps.shape[1:]
    order, width = got.shape
    z, c = lax.axis_index("z"), lax.axis_index("c")
    line = lax.dynamic_index_in_dim(maps, z, 0, keepdims=False).reshape(ns // 2, 2, corners)
    iota = lax.broadcasted_iota(jnp.int32, (1, order), 1)
    parts = jnp.concatenate(split3(got), axis=1)

    def rows_of(which):
        names = lax.dynamic_index_in_dim(line, which, 1, keepdims=False).reshape(ns // 2 * corners)
        picks = (names[:, None] == iota).astype(jnp.bfloat16)
        wide = jnp.dot(picks, parts, preferred_element_type=jnp.float32)
        return wide[:, :width] + wide[:, width : 2 * width] + wide[:, 2 * width :]

    own = rows_of(c)
    other = rows_of(1 - c)
    back = lax.ppermute(other, "c", [(0, 1), (1, 0)])
    return jnp.concatenate([jnp.where(c == 0, own, back), jnp.where(c == 0, back, own)], axis=1)


def body(loads, dual_op, dirichlet, corner_coupling, corner_map, coarse_inverse):
    at_z, at_s = lax.axis_index("z"), lax.axis_index(SY)
    ends = [at_z > 0, at_z + 1 < lax.axis_size("z"), at_s > 0, at_s + 1 < lax.axis_size(SY)]
    flags = jnp.stack(ends).astype(jnp.int32)
    order, cases = loads.shape
    field = (order, cases)
    sends = [(FACE + 2 * EDGE, cases)] * 2 + [(FACE, cases)] * 2
    edges = [(2 * EDGE, cases)] * 2
    groups, targets = lax.axis_size(GATHER), lax.axis_size(SCATTER)
    few = (8, cases)
    parts = (pltpu.VMEM((order, 2 * cases), jnp.bfloat16),)
    coupling_t = corner_coupling.T
    wide_t = jnp.concatenate([coupling_t, coupling_t, coupling_t], axis=1)
    big = 4 * order * order * cases

    maps, blocks = coarse_columns(corner_map, coarse_inverse)
    r = loads
    u, *out = call(smooth_kernel, [field, *sends], [r, dirichlet], 0, parts, big)
    blocks, *out = lax.optimization_barrier((blocks, *out))
    got = lax.all_to_all(blocks, SY, 0, 0).reshape(coarse_inverse.shape[1], -1)

    def exchange(up, down, left, right):
        from_down, from_up = shifted(up, True, 1), shifted(down, True, -1)
        from_left, from_right = shifted(right, False, 1), shifted(left, False, -1)
        left, right = call(forward_kernel, edges, [from_down, from_up])
        return from_down, from_up, from_left, from_right, shifted(right, False, 1), shifted(left, False, -1)

    def spread_of(value, received, dots):
        return call(
            spread_kernel,
            [field, field, (groups, 24, cases)],
            [flags, value, *received, dual_op, corner_coupling, dots],
            1,
            parts,
            big,
        )

    def image_of(first_step, block, sent, local, last):
        got = lax.all_to_all(sent, GATHER, 0, 0)
        (sent,) = call(coarse_kernel, [(targets, 24, cases)], [got, block])
        got = lax.all_to_all(sent, SCATTER, 0, 0)
        return call(
            functools.partial(image_kernel, first_step),
            [field, *sends, few],
            [got, local, wide_t, last],
            0,
            (pltpu.VMEM((48, cases), jnp.float32),),
        )

    received = exchange(*out)
    zeros = jnp.zeros(few, jnp.float32)
    yu, local, sent = spread_of(u, received, zeros)
    block = coarse_block(maps, got)
    image, *out, scalars = image_of(True, block, sent, local, zeros)
    received = exchange(*out)
    w, dots, m, *out = call(
        start_kernel, [field, few, field, *sends], [flags, image, *received, r, u, dirichlet], 1, parts, big
    )
    x = jnp.zeros(field, jnp.float32)
    p, s, q, yq, z = u, w, m, None, w
    for step in range(ITERS - 1):
        received = exchange(*out)
        ym, local, sent = spread_of(m, received, dots)
        image, *out, scalars = image_of(step == 0, block, sent, local, scalars)
        u, r, x, p, s, q, yu, yq = call(
            update_kernel,
            [field] * 8,
            [scalars, u, w, r, x, p, s, q, m, yu, ym if step == 0 else yq, ym],
        )
        if step + 2 == ITERS:
            (sent,) = call(ends_kernel, [(lax.axis_size(ALL), 2, cases)], [scalars, u, r, w, z, yu, image])
            sums = lax.all_to_all(sent, ALL, 0, 0)
            received = exchange(*out)
            break
        received = exchange(*out)
        z, w, dots, m, *out = call(
            step_kernel,
            [field, field, few, field, *sends],
            [flags, image, *received, z, w, r, u, scalars, dirichlet],
            1,
            parts,
            big,
        )
    (n,) = call(finish_kernel, [field], [flags, image, *received], 1)
    last_alpha, last_gamma, last_beta = scalars[0:1], scalars[1:2], scalars[2:3]
    sums = jnp.sum(sums, axis=0)
    gamma, delta = sums[0:1], sums[1:2]
    beta = gamma / last_gamma
    alpha = gamma / (delta - beta * gamma / last_alpha)
    w = w - last_alpha * (n + last_beta * z)
    return x + alpha * (u + beta * p), r - alpha * (w + beta * s)


def solution(mesh):
    nz, ns = mesh.shape["sx"], mesh.shape["sy"]
    fine = Mesh(mesh.devices.reshape(nz, 4, ns // 8, 2), ALL)
    in_specs = (P("z", SY),) * 5 + (P(SY, None),)
    out_specs = (P("z", SY), P("z", SY))
    return jax.shard_map(body, mesh=fine, in_specs=in_specs, out_specs=out_specs, check_vma=False)
```

```python
import functools
import math

import jax
import jax.numpy as jnp
from jax import lax
from jax.experimental import pallas as pl
from jax.experimental.pallas import tpu as pltpu
from jax.sharding import Mesh
from jax.sharding import PartitionSpec as P

FACE = 320
EDGE = 64
TILE = 256
ITERS = 4
HALF = 0.5
HIGH = lax.Precision.HIGHEST
SY = ("y", "x", "c")
ALL = ("z", "y", "x", "c")
GATHER = ("z", "c")
SCATTER = ("y", "x")


def shifted(value, step):
    nz, ns = lax.axis_size("z"), lax.axis_size(SY)
    pairs = [(z * ns + k, (z + step) % nz * ns + k) for z in range(nz) for k in range(ns)]
    return lax.ppermute(value, ALL, pairs)


def swapped(value, first):
    nz, ns = lax.axis_size("z"), lax.axis_size(SY)
    pairs = []
    for z in range(nz):
        for k in range(ns):
            other = k + 1 if k % 2 == first else k - 1
            target = z * ns + other if 0 <= other < ns else (z ^ 1) * ns + k
            pairs.append((z * ns + k, target))
    return lax.ppermute(value, ALL, pairs)


def call(kernel, shapes, operands, smem=0, scratch=(), flops=1_000_000):
    out_shape = [jax.ShapeDtypeStruct(shape, jnp.float32) for shape in shapes]
    moved = 4 * sum(math.prod(shape) for shape in shapes) + sum(x.size * x.dtype.itemsize for x in operands)
    return pl.pallas_call(
        kernel,
        out_shape=out_shape,
        in_specs=[pl.BlockSpec(memory_space=pltpu.SMEM)] * smem
        + [pl.BlockSpec(memory_space=pltpu.VMEM)] * (len(operands) - smem),
        out_specs=[pl.BlockSpec(memory_space=pltpu.VMEM)] * len(shapes),
        scratch_shapes=list(scratch),
        compiler_params=pltpu.CompilerParams(vmem_limit_bytes=6 * 1024 * 1024),
        cost_estimate=pl.CostEstimate(flops=flops, bytes_accessed=moved, transcendentals=0),
    )(*operands)


def put_parts(parts_ref, rows, value):
    cases = value.shape[1]
    high = value.astype(jnp.bfloat16)
    parts_ref[rows, :cases] = high
    parts_ref[rows, cases:] = (value - high.astype(jnp.float32)).astype(jnp.bfloat16)


def multiplied(matrix_ref, parts_ref, out_ref, extra=None):
    order, cases = out_ref.shape

    def tile(i, carry):
        rows = pl.ds(pl.multiple_of(i * TILE, TILE), TILE)
        wide = jnp.dot(matrix_ref[rows, :], parts_ref[...], preferred_element_type=jnp.float32)
        total = wide[:, :cases] + wide[:, cases:]
        if extra is not None:
            total = total + extra(rows)
        out_ref[rows, :] = total
        return carry

    lax.fori_loop(0, order // TILE, tile, 0)


def put_sends(flags_ref, field_ref, up_ref, down_ref, first_ref, second_ref):
    up_ref[0:320, :] = field_ref[320:640, :]
    up_ref[320:448, :] = field_ref[1408:1536, :]
    down_ref[0:320, :] = field_ref[0:320, :]
    down_ref[320:448, :] = field_ref[1280:1408, :]
    first_ref[...] = field_ref[pl.ds(pl.multiple_of(640 + flags_ref[4] * FACE, 64), 320), :]
    second_ref[...] = field_ref[pl.ds(pl.multiple_of(960 - flags_ref[4] * FACE, 64), 320), :]


def forward_kernel(flags_ref, from_down_ref, from_up_ref, first_ref, second_ref):
    even = flags_ref[4] == 1
    for rows, ref in ((slice(0, 64), from_up_ref), (slice(64, 128), from_down_ref)):
        left, right = ref[320:384, :], ref[384:448, :]
        first_ref[rows, :] = jnp.where(even, right, left)
        second_ref[rows, :] = jnp.where(even, left, right)


def with_incoming(flags_ref, received_refs, visit, carry):
    down_ref, up_ref, first_ref, second_ref, edge_first_ref, edge_second_ref = received_refs
    down, up, left, right, even = (flags_ref[k] == 1 for k in range(5))
    pieces = (
        (0, 320, down, down_ref, down_ref, 0),
        (320, 640, up, up_ref, up_ref, 0),
        (640, 960, left, second_ref, first_ref, 0),
        (960, 1280, right, first_ref, second_ref, 0),
        (1280, 1344, jnp.logical_and(left, down), edge_second_ref, edge_first_ref, 64),
        (1344, 1408, jnp.logical_and(right, down), edge_first_ref, edge_second_ref, 64),
        (1408, 1472, jnp.logical_and(left, up), edge_second_ref, edge_first_ref, 0),
        (1472, 1536, jnp.logical_and(right, up), edge_first_ref, edge_second_ref, 0),
    )
    for low, high, there, if_even, if_odd, start in pieces:

        def chunk(i, carry, low=low, there=there, if_even=if_even, if_odd=if_odd, start=start):
            source = pl.ds(pl.multiple_of(start + i * 64, 64), 64)
            theirs = if_even[source, :]
            if if_odd is not if_even:
                theirs = jnp.where(even, theirs, if_odd[source, :])
            rows = pl.ds(pl.multiple_of(low + i * 64, 64), 64)
            return visit(rows, jnp.where(there, theirs, 0.0), carry)

        carry = lax.fori_loop(0, (high - low) // 64, chunk, carry)
    return carry


def smooth_kernel(flags_ref, field_ref, matrix_ref, out_ref, *rest):
    *send_refs, parts_ref = rest
    put_parts(parts_ref, slice(None), field_ref[...])
    multiplied(matrix_ref, parts_ref, out_ref)
    put_sends(flags_ref, out_ref, *send_refs)


def spread_kernel(
    flags_ref, field_ref, z1, z2, s1, s2, d1, d2, matrix_ref, coupling_ref, dots_ref,
    spread_ref, local_ref, sent_ref, parts_ref,
):
    cases = spread_ref.shape[1]
    received_refs = z1, z2, s1, s2, d1, d2

    def visit(rows, theirs, carry):
        value = field_ref[rows, :] + HALF * theirs
        spread_ref[rows, :] = value
        put_parts(parts_ref, rows, value)
        return carry

    with_incoming(flags_ref, received_refs, visit, 0)
    wide = jnp.dot(coupling_ref[...], parts_ref[...], preferred_element_type=jnp.float32)
    corner = wide[:, :cases] + wide[:, cases:]
    for k in range(sent_ref.shape[0]):
        sent_ref[k, 0:16, :] = corner
        sent_ref[k, 16:24, :] = dots_ref[...]
    multiplied(matrix_ref, parts_ref, local_ref)


def coarse_kernel(got_ref, block_ref, sent_ref):
    count = got_ref.shape[0]
    parts = jnp.concatenate([got_ref[k, 0:16, :] for k in (*range(0, count, 2), *range(1, count, 2))], axis=0)
    sums = got_ref[0, 16:24, :]
    for k in range(1, count):
        sums = sums + got_ref[k, 16:24, :]
    product = jnp.dot(block_ref[...], parts, precision=HIGH, preferred_element_type=jnp.float32)
    for k in range(sent_ref.shape[0]):
        sent_ref[k, 0:16, :] = product[16 * k : 16 * k + 16]
        sent_ref[k, 16:24, :] = sums


def image_kernel(
    first_step, flags_ref, got_ref, local_ref, coupling_ref, last_ref,
    image_ref, z1, z2, s1, s2, scalars_ref, wide_ref,
):
    send_refs = z1, z2, s1, s2
    total = got_ref[0]
    for k in range(1, got_ref.shape[0]):
        total = total + got_ref[k]
    picked = total[0:16]
    high = picked.astype(jnp.bfloat16).astype(jnp.float32)
    rest = picked - high
    middle = rest.astype(jnp.bfloat16).astype(jnp.float32)
    wide_ref[0:16, :] = high
    wide_ref[16:32, :] = middle
    wide_ref[32:48, :] = rest - middle
    pieces = wide_ref[...].astype(jnp.bfloat16)
    order = image_ref.shape[0]
    gamma, delta = total[16:17], total[17:18]
    if first_step:
        alpha = gamma / delta
        beta = jnp.zeros_like(gamma)
    else:
        beta = gamma / last_ref[1:2, :]
        alpha = gamma / (delta - beta * gamma / last_ref[0:1, :])
    scalars_ref[0:1, :] = alpha
    scalars_ref[1:2, :] = gamma
    scalars_ref[2:3, :] = beta
    scalars_ref[3:8, :] = jnp.zeros((5,) + gamma.shape[1:], jnp.float32)
    image_ref[...] = local_ref[...] + jnp.dot(coupling_ref[...], pieces, preferred_element_type=jnp.float32)
    put_sends(flags_ref, image_ref, *send_refs)


def inner(first, second):
    return jnp.sum(first * second, axis=0, keepdims=True)


def start_kernel(
    flags_ref, image_ref, z1, z2, s1, s2, d1, d2, r_ref, u_ref, matrix_ref,
    w_ref, dots_ref, m_ref, a1, a2, b1, b2, parts_ref,
):
    received_refs = z1, z2, s1, s2, d1, d2
    send_refs = a1, a2, b1, b2

    def visit(rows, theirs, delta):
        value = image_ref[rows, :] + HALF * theirs
        w_ref[rows, :] = value
        put_parts(parts_ref, rows, value)
        return delta + inner(value, u_ref[rows, :])

    delta = with_incoming(flags_ref, received_refs, visit, jnp.zeros((1, w_ref.shape[1]), jnp.float32))
    dots_ref[...] = jnp.zeros_like(dots_ref)
    dots_ref[0:1, :] = inner(r_ref[...], u_ref[...])
    dots_ref[1:2, :] = delta
    multiplied(matrix_ref, parts_ref, m_ref)
    put_sends(flags_ref, m_ref, *send_refs)


def step_kernel(
    flags_ref, image_ref, z1, z2, s1, s2, d1, d2, z_ref, w_ref, r_ref, u_ref, scalars_ref, matrix_ref,
    new_z_ref, new_w_ref, dots_ref, m_ref, a1, a2, b1, b2, parts_ref,
):
    alpha, beta = scalars_ref[0:1, :], scalars_ref[2:3, :]
    received_refs = z1, z2, s1, s2, d1, d2
    send_refs = a1, a2, b1, b2

    def visit(rows, theirs, delta):
        z = image_ref[rows, :] + HALF * theirs + beta * z_ref[rows, :]
        new_z_ref[rows, :] = z
        value = w_ref[rows, :] - alpha * z
        new_w_ref[rows, :] = value
        put_parts(parts_ref, rows, value)
        return delta + inner(value, u_ref[rows, :])

    delta = with_incoming(flags_ref, received_refs, visit, jnp.zeros_like(alpha))
    dots_ref[...] = jnp.zeros_like(dots_ref)
    dots_ref[0:1, :] = inner(r_ref[...], u_ref[...])
    dots_ref[1:2, :] = delta
    multiplied(matrix_ref, parts_ref, m_ref)
    put_sends(flags_ref, m_ref, *send_refs)


def update_kernel(
    scalars_ref, u_ref, w_ref, r_ref, x_ref, p_ref, s_ref, q_ref, m_ref, yu_ref, yq_ref, ym_ref,
    new_u, new_r, new_x, new_p, new_s, new_q, new_yu, new_yq,
):
    alpha, beta = scalars_ref[0:1, :], scalars_ref[2:3, :]

    def tile(i, carry):
        rows = pl.ds(pl.multiple_of(i * TILE, TILE), TILE)
        u = u_ref[rows, :]
        p = u + beta * p_ref[rows, :]
        s = w_ref[rows, :] + beta * s_ref[rows, :]
        q = m_ref[rows, :] + beta * q_ref[rows, :]
        yq = ym_ref[rows, :] + beta * yq_ref[rows, :]
        new_p[rows, :] = p
        new_s[rows, :] = s
        new_q[rows, :] = q
        new_yq[rows, :] = yq
        new_x[rows, :] = x_ref[rows, :] + alpha * p
        new_r[rows, :] = r_ref[rows, :] - alpha * s
        new_u[rows, :] = u - alpha * q
        new_yu[rows, :] = yu_ref[rows, :] - alpha * yq
        return carry

    lax.fori_loop(0, u_ref.shape[0] // TILE, tile, 0)


def ends_kernel(scalars_ref, u_ref, r_ref, w_ref, z_ref, yu_ref, image_ref, sent_ref):
    alpha, beta = scalars_ref[0:1, :], scalars_ref[2:3, :]
    u = u_ref[...]
    gamma = inner(r_ref[...], u)
    delta = inner(u, w_ref[...] - (alpha * beta) * z_ref[...]) - alpha * inner(yu_ref[...], image_ref[...])
    both = jnp.concatenate([gamma, delta], axis=0)
    sent_ref[...] = jnp.broadcast_to(both[None], sent_ref.shape)


def finish_kernel(flags_ref, image_ref, z1, z2, s1, s2, d1, d2, out_ref):
    received_refs = z1, z2, s1, s2, d1, d2

    def visit(rows, theirs, carry):
        out_ref[rows, :] = image_ref[rows, :] + HALF * theirs
        return carry

    with_incoming(flags_ref, received_refs, visit, 0)


def rounded_part(value):
    return lax.reduce_precision(value, exponent_bits=8, mantissa_bits=7)


def split3(value):
    high = rounded_part(value)
    middle = rounded_part(value - high)
    low = value - high - middle
    return high.astype(jnp.bfloat16), middle.astype(jnp.bfloat16), low.astype(jnp.bfloat16)


def picked_product(left_f32, onehot):
    rows = left_f32.shape[0]
    product = jnp.dot(jnp.concatenate(split3(left_f32), axis=0), onehot, preferred_element_type=jnp.float32)
    return product[:rows] + product[rows : 2 * rows] + product[2 * rows :]


def coarse_columns(corner_map, coarse_inverse):
    nz, ns = lax.axis_size("z"), lax.axis_size(SY)
    corners = corner_map.shape[1]
    rows, order = coarse_inverse.shape
    mine = jnp.pad(corner_map.astype(jnp.float32), ((0, 0), (0, 128 - corners)))
    sent = jnp.broadcast_to(mine[None], (nz * ns, 1, 128))
    maps = lax.all_to_all(sent, ALL, 0, 0)[:, 0, :corners].astype(jnp.int32).reshape(nz, ns, corners)
    columns = maps.transpose(1, 0, 2).reshape(ns * nz * corners)
    iota = lax.broadcasted_iota(jnp.int32, (order, 1), 0)
    onehot = (iota == columns[None, :]).astype(jnp.bfloat16)
    chosen = picked_product(coarse_inverse, onehot)
    return maps, chosen.reshape(rows, ns, nz * corners).transpose(1, 0, 2)


def coarse_block(maps, got):
    ns, corners = maps.shape[1:]
    order, width = got.shape
    z, c = lax.axis_index("z"), lax.axis_index("c")
    line = lax.dynamic_index_in_dim(maps, z, 0, keepdims=False).reshape(ns // 2, 2, corners)
    iota = lax.broadcasted_iota(jnp.int32, (1, order), 1)
    parts = jnp.concatenate(split3(got), axis=1)

    def rows_of(which):
        names = lax.dynamic_index_in_dim(line, which, 1, keepdims=False).reshape(ns // 2 * corners)
        picks = (names[:, None] == iota).astype(jnp.bfloat16)
        wide = jnp.dot(picks, parts, preferred_element_type=jnp.float32)
        return wide[:, :width] + wide[:, width : 2 * width] + wide[:, 2 * width :]

    own = rows_of(c)
    other = rows_of(1 - c)
    back = lax.ppermute(other, "c", [(0, 1), (1, 0)])
    return jnp.concatenate([jnp.where(c == 0, own, back), jnp.where(c == 0, back, own)], axis=1)


def body(loads, dual_op, dirichlet, corner_coupling, corner_map, coarse_inverse):
    at_z, at_s = lax.axis_index("z"), lax.axis_index(SY)
    ends = [at_z > 0, at_z + 1 < lax.axis_size("z"), at_s > 0, at_s + 1 < lax.axis_size(SY), at_s % 2 == 0]
    flags = jnp.stack(ends).astype(jnp.int32)
    order, cases = loads.shape
    field = (order, cases)
    sends = [(FACE + 2 * EDGE, cases)] * 2 + [(FACE, cases)] * 2
    edges = [(2 * EDGE, cases)] * 2
    groups, targets = lax.axis_size(GATHER), lax.axis_size(SCATTER)
    few = (8, cases)
    parts = (pltpu.VMEM((order, 2 * cases), jnp.bfloat16),)
    coupling_t = corner_coupling.T
    wide_t = jnp.concatenate([coupling_t, coupling_t, coupling_t], axis=1)
    big = 4 * order * order * cases

    maps, blocks = coarse_columns(corner_map, coarse_inverse)
    r = loads
    u, *out = call(smooth_kernel, [field, *sends], [flags, r, dirichlet], 1, parts, big)
    blocks, *out = lax.optimization_barrier((blocks, *out))
    got = lax.all_to_all(blocks, SY, 0, 0).reshape(coarse_inverse.shape[1], -1)

    def exchange(up, down, first, second, held=None):
        from_down, from_up = shifted(up, 1), shifted(down, -1)
        first, second = swapped(first, 0), swapped(second, 1)
        edge_first, edge_second = call(forward_kernel, edges, [flags, from_down, from_up], 1)
        if held is not None:
            held, edge_first, edge_second = lax.optimization_barrier((held, edge_first, edge_second))
            sums = lax.all_to_all(held, ALL, 0, 0)
            return (from_down, from_up, first, second, swapped(edge_first, 0), swapped(edge_second, 1)), sums
        return from_down, from_up, first, second, swapped(edge_first, 0), swapped(edge_second, 1)

    def spread_of(value, received, dots):
        return call(
            spread_kernel,
            [field, field, (groups, 24, cases)],
            [flags, value, *received, dual_op, corner_coupling, dots],
            1,
            parts,
            big,
        )

    def image_of(first_step, block, sent, local, last):
        got = lax.all_to_all(sent, GATHER, 0, 0)
        (sent,) = call(coarse_kernel, [(targets, 24, cases)], [got, block])
        got = lax.all_to_all(sent, SCATTER, 0, 0)
        return call(
            functools.partial(image_kernel, first_step),
            [field, *sends, few],
            [flags, got, local, wide_t, last],
            1,
            (pltpu.VMEM((48, cases), jnp.float32),),
        )

    received = exchange(*out)
    zeros = jnp.zeros(few, jnp.float32)
    yu, local, sent = spread_of(u, received, zeros)
    block = coarse_block(maps, got)
    image, *out, scalars = image_of(True, block, sent, local, zeros)
    received = exchange(*out)
    w, dots, m, *out = call(
        start_kernel, [field, few, field, *sends], [flags, image, *received, r, u, dirichlet], 1, parts, big
    )
    x = jnp.zeros(field, jnp.float32)
    p, s, q, yq, z = u, w, m, None, w
    for step in range(ITERS - 1):
        received = exchange(*out)
        ym, local, sent = spread_of(m, received, dots)
        image, *out, scalars = image_of(step == 0, block, sent, local, scalars)
        u, r, x, p, s, q, yu, yq = call(
            update_kernel,
            [field] * 8,
            [scalars, u, w, r, x, p, s, q, m, yu, ym if step == 0 else yq, ym],
        )
        if step + 2 == ITERS:
            (sent,) = call(ends_kernel, [(lax.axis_size(ALL), 2, cases)], [scalars, u, r, w, z, yu, image])
            received, sums = exchange(*out, held=sent)
            break
        received = exchange(*out)
        z, w, dots, m, *out = call(
            step_kernel,
            [field, field, few, field, *sends],
            [flags, image, *received, z, w, r, u, scalars, dirichlet],
            1,
            parts,
            big,
        )
    (n,) = call(finish_kernel, [field], [flags, image, *received], 1)
    last_alpha, last_gamma, last_beta = scalars[0:1], scalars[1:2], scalars[2:3]
    sums = jnp.sum(sums, axis=0)
    gamma, delta = sums[0:1], sums[1:2]
    beta = gamma / last_gamma
    alpha = gamma / (delta - beta * gamma / last_alpha)
    w = w - last_alpha * (n + last_beta * z)
    return x + alpha * (u + beta * p), r - alpha * (w + beta * s)


def solution(mesh):
    nz, ns = mesh.shape["sx"], mesh.shape["sy"]
    fine = Mesh(mesh.devices.reshape(nz, 4, ns // 8, 2), ALL)
    in_specs = (P("z", SY),) * 5 + (P(SY, None),)
    out_specs = (P("z", SY), P("z", SY))
    return jax.shard_map(body, mesh=fine, in_specs=in_specs, out_specs=out_specs, check_vma=False)
```
